512 devices in a mesh: head: 16 (over y, x), seq: 32 (over z, core).
Axes of the slice: x: 4, y: 4, z: 16, core: 2. Of those that a mesh axis runs over, the one named last changes fastest.
Arguments:
- features: bfloat16 [3072, 8192], P('head', 'seq'), may hold values from -12 to 12
- w_query: bfloat16 [3072, 3072], P('head'), may hold values from -0.109375 to 0.109375
- w_key: bfloat16 [3072, 3072], P('head'), may hold values from -0.109375 to 0.109375
- w_value: bfloat16 [3072, 3072], P('head'), may hold values from -0.109375 to 0.109375
- rates: float32 [8192, 48], P('seq', 'head'), may hold values from 0 to 0.03125, as said below
- scene_bounds: int32 [32, 2], P('seq'), may hold values from 0 to 256, as said below
- w_init: float32 [48, 64, 64], P('head'), may hold values from -0.18 to 0.18
- out_gain: float32 [3072], P('head'), may hold values from 0.5 to 1.5
Outputs:
- mixed: bfloat16 [3072, 8192], P('head', 'seq')
The draws below stay inside these ranges and needn't reach their ends.
Inputs may be any that keep to these rules, and one draw needn't show every extreme that they name: Per slot and head, 0 < rate <= 2 / 64; the rates of a mini-batch sum to at most 2, and some mini-batches reach the bound for every head. `scene_bounds`: each shard's row is (start, end) with start < 256 // 8 (or 0) and end > 256 - 256 // 8 (or 256); some shard has start 0 and end 256.
All inputs are finite; a program needn't handle non-finite values.
Results may differ from the reference program's by a relative error of at most 0.0085.
Values may be sent and summed in bfloat16 or wider, within the bound.
A program may use at most 64 MiB of HBM per device.

```python
import math
import jax
import jax.numpy as jnp
from jax import lax

HEADS = 48
HEAD_SIZE = 64
MINI = 64
TOK_DEV = 256
D = 3072
SHARDS = 32
TOKENS = 8192


def draw_features(key, part):
    key_collection = jax.random.split(key, 5)
    block_list = TOKENS // MINI
    jitter = jnp.clip(jax.random.normal(key_collection[0], (D, TOKENS), jnp.float32), -4.0, 4.0)
    strength = jax.random.uniform(key_collection[4], (block_list,), jnp.float32, 1.0, 2.5)
    common = jnp.clip(jax.random.normal(key_collection[1], (D, 1), jnp.float32), -3.0, 3.0)
    shard_dirs = jnp.clip(jax.random.normal(key_collection[2], (D, TOKENS // TOK_DEV), jnp.float32), -3.0, 3.0)
    block_dirs = jnp.clip(jax.random.normal(key_collection[3], (D, block_list), jnp.float32), -3.0, 3.0)
    shared_blocks = 0.6 * common + 0.5 * jnp.repeat(shard_dirs, TOK_DEV // MINI, axis=1) + 0.7 * block_dirs
    shared_blocks = shared_blocks * strength[None, :]
    shared = jnp.repeat(shared_blocks, MINI, axis=1)
    return jnp.clip(jitter + shared, -12.0, 12.0).astype(jnp.bfloat16)


def draw_rates(key, part):
    key_collection = jax.random.split(key, 4)
    block_list = TOKENS // MINI
    upper_limit = 2.0 / MINI
    level = jnp.exp(jax.random.uniform(key_collection[0], (HEADS,), jnp.float32, math.log(0.15), 0.0))
    shard_factor = jax.random.uniform(key_collection[1], (TOKENS // TOK_DEV, HEADS), jnp.float32, 0.5, 1.0)
    token_factor = jax.random.uniform(key_collection[2], (TOKENS, HEADS), jnp.float32, 0.75, 1.0)
    span_labels = jax.random.randint(key_collection[3], (4,), 0, block_list)
    block_numbers = jnp.arange(TOKENS, dtype=jnp.int32) // MINI
    scene_span = jnp.any(block_numbers[:, None] == span_labels[None, :], axis=1)
    spread = jnp.repeat(shard_factor, TOK_DEV, axis=0)
    draw_level = upper_limit * level[None, :] * spread * token_factor
    draw_level = jnp.where(scene_span[:, None], upper_limit, draw_level)
    return jnp.minimum(draw_level, upper_limit).astype(jnp.float32)


def draw_scene_bounds(key, part):
    first_key, second_key = jax.random.split(key)
    margin = max(TOK_DEV // 8, 1)
    starts = jax.random.randint(first_key, (SHARDS,), 0, margin)
    ends = TOK_DEV - jax.random.randint(second_key, (SHARDS,), 0, margin)
    leading = jnp.arange(SHARDS) == 0
    starts = jnp.where(leading, 0, starts)
    ends = jnp.where(leading, TOK_DEV, ends)
    return jnp.stack([starts, ends], axis=1).astype(jnp.int32)


def block_scale(stream_key, shape, shards, low, high):
    loudness = 1.0
    for axis_at, blocks in shards:
        draws = jax.random.uniform(jax.random.fold_in(jax.random.fold_in(stream_key, 6), axis_at), (blocks,), jnp.float32, low / len(shards), high / len(shards))
        loudness = loudness * jnp.repeat(jnp.exp(draws), shape[axis_at] // blocks).reshape((-1,) + (1,) * (len(shape) - 1 - axis_at))
    return loudness


def centred(own_key, dims, scale, limit, pieces=(), kind=jnp.bfloat16):
    gain = block_scale(own_key, dims, pieces, -0.22, 0.18) if pieces else 1.0
    values = jax.random.normal(own_key, dims, jnp.float32) * scale * gain
    return jnp.minimum(jnp.maximum(values, -limit), limit).astype(kind)


def setup_inputs(seed: int = 0) -> dict:
    key_of = jax.random.split(jax.random.key(seed), 9)
    features = draw_features(jax.random.fold_in(key_of[8], 71), 0)
    w_query = centred(key_of[1], (D, D), D ** -0.5, 0.109375, ((0, 16),))
    w_key = centred(key_of[2], (D, D), D ** -0.5, 0.109375, ((0, 16),))
    w_value = centred(key_of[3], (D, D), D ** -0.5, 0.109375, ((0, 16),))
    rates = draw_rates(jax.random.fold_in(key_of[8], 71), 0)
    scene_bounds = draw_scene_bounds(jax.random.fold_in(key_of[8], 71), 0)
    w_init = centred(key_of[6], (HEADS, HEAD_SIZE, HEAD_SIZE), 0.03, 0.18, ((0, 16),), jnp.float32)
    out_gain = jnp.clip(1.0 + 0.1 * jax.random.normal(key_of[7], (D,), jnp.float32), 0.5, 1.5)
    return dict(features=features, w_query=w_query, w_key=w_key, w_value=w_value, rates=rates, scene_bounds=scene_bounds, w_init=w_init, out_gain=out_gain)


highest = lax.Precision.HIGHEST

def unit_rows(values):
    width = values.shape[-1]
    scale = lax.rsqrt(lax.optimization_barrier(jnp.mean(values * values, axis=-1, keepdims=True)) + 1e-06)
    return values * scale / math.sqrt(width)

def layer_norm(values):
    centre = values - lax.optimization_barrier(jnp.mean(values, axis=-1, keepdims=True))
    return centre * lax.rsqrt(lax.optimization_barrier(jnp.mean(centre * centre, axis=-1, keepdims=True)) + 1e-05)

def run_chain(query_rows, key_rows, value_rows, eta_rows, w_start):
    block_list = query_rows.shape[0] // MINI
    width = query_rows.shape[1]
    query_blk = query_rows.reshape(block_list, MINI, width)
    key_blk = key_rows.reshape(block_list, MINI, width)
    value_blk = value_rows.reshape(block_list, MINI, width)
    eta_blk = eta_rows.reshape(block_list, MINI)
    lower = jnp.tril(jnp.ones((MINI, MINI), jnp.float32))

    def advance(state, block):
        qb, kb, vb, eb = block
        scores = jnp.dot(qb, kb.T, precision=highest) * eb[None, :] * lower
        error = jnp.dot(kb, state, precision=highest) - vb
        output = jnp.dot(qb, state, precision=highest) - jnp.dot(scores, error, precision=highest)
        state = state - jnp.dot(kb.T, eb[:, None] * error, precision=highest)
        return (state, output)
    final_state, outputs = lax.scan(advance, w_start, (query_blk, key_blk, value_blk, eta_blk))
    return outputs.reshape(block_list * MINI, width)

def reference(features, w_query, w_key, w_value, rates, scene_bounds, w_init, out_gain):
    queries = jnp.dot(w_query, features, preferred_element_type=jnp.float32).astype(jnp.bfloat16).T
    keys_all = jnp.dot(w_key, features, preferred_element_type=jnp.float32).astype(jnp.bfloat16).T
    values_all = jnp.dot(w_value, features, preferred_element_type=jnp.float32).astype(jnp.bfloat16).T
    slots = jnp.arange(TOKENS, dtype=jnp.int32)
    shard_ids = (slots // TOK_DEV).astype(jnp.int32)
    local_ids = (slots % TOK_DEV).astype(jnp.int32)
    bounds = scene_bounds[shard_ids]
    live = ((local_ids >= bounds[:, 0]) & (local_ids < bounds[:, 1])).astype(jnp.float32)
    eta = rates * live[:, None]
    query_heads = unit_rows(queries.astype(jnp.float32).reshape(TOKENS, HEADS, HEAD_SIZE))
    key_heads = unit_rows(keys_all.astype(jnp.float32).reshape(TOKENS, HEADS, HEAD_SIZE))
    value_heads = values_all.astype(jnp.float32).reshape(TOKENS, HEADS, HEAD_SIZE)
    chains = jax.vmap(run_chain, in_axes=(1, 1, 1, 1, 0), out_axes=1)
    forward_out = chains(query_heads, key_heads, value_heads, eta, w_init)
    backward_out = chains(query_heads[::-1], key_heads[::-1], value_heads[::-1], eta[::-1], w_init)[::-1]
    joined = (layer_norm(forward_out) + layer_norm(backward_out)).reshape(TOKENS, D)
    return (joined * out_gain[None, :] * live[:, None]).T.astype(jnp.bfloat16)
```

```python
import functools
import math

import jax
import jax.numpy as jnp
from jax import lax
from jax.experimental import pallas as pl
from jax.experimental.pallas import tpu as pltpu
from jax.sharding import PartitionSpec as P

MINI = 64
MESH = pl.DeviceIdType.MESH
highest = lax.Precision.HIGHEST
VMEM = pltpu.VMEM


def dot(a, b):
    return jnp.dot(a, b, precision=highest, preferred_element_type=jnp.float32)


def gather_kernel(n, x_ref, out_ref, own_sem, send_sem, recv_sem):
    me = lax.axis_index("head")
    barrier = pltpu.get_barrier_semaphore()
    for off in range(1, n):
        peer = lax.rem(me + off, n)
        pl.semaphore_signal(barrier, inc=1, device_id={"head": peer}, device_id_type=MESH)
    own = pltpu.make_async_copy(x_ref, out_ref.at[me], own_sem)
    own.start()
    pl.semaphore_wait(barrier, n - 1)

    def copy(off, slot, peer):
        return pltpu.make_async_remote_copy(
            src_ref=x_ref,
            dst_ref=out_ref.at[slot],
            send_sem=send_sem.at[off],
            recv_sem=recv_sem.at[off],
            device_id={"head": peer},
            device_id_type=MESH,
        )

    for off in range(1, n):
        copy(off, me, lax.rem(me + off, n)).start()
    own.wait()
    for off in range(1, n):
        source = lax.rem(me - off + n, n)
        copy(off, source, source).wait_recv()
    for off in range(1, n):
        copy(off, me, lax.rem(me + off, n)).wait_send()


def gather(x, n):
    return pl.pallas_call(
        functools.partial(gather_kernel, n),
        out_shape=jax.ShapeDtypeStruct((n,) + x.shape, x.dtype),
        in_specs=[pl.BlockSpec(memory_space=pl.ANY)],
        out_specs=pl.BlockSpec(memory_space=pl.ANY),
        scratch_shapes=[
            pltpu.SemaphoreType.DMA,
            pltpu.SemaphoreType.DMA((n,)),
            pltpu.SemaphoreType.DMA((n,)),
        ],
        compiler_params=pltpu.CompilerParams(collective_id=0, has_side_effects=True),
        name="gather_features",
    )(x)


def homog(pair, low):
    return jnp.concatenate([pair, low], axis=0)


def iota2(shape, axis):
    return lax.broadcasted_iota(jnp.int32, shape, axis)


def low_rows(width):
    rows = iota2((width, 2 * width), 0)
    cols = iota2((width, 2 * width), 1)
    return (cols == rows + width).astype(jnp.float32)


def live_row(bounds_ref, length):
    slots = iota2((1, length), 1)
    return ((slots >= bounds_ref[0, 0]) & (slots < bounds_ref[0, 1])).astype(jnp.float32)


def local_kernel(heads, width, bounds_ref, x_ref, wq_ref, wk_ref, wv_ref, rates_ref, terms_ref, maps_ref):
    length = x_ref.shape[1]
    blocks = length // MINI
    x = x_ref[...]

    def project(ref):
        total = jnp.dot(ref[...], x, preferred_element_type=jnp.float32)
        return total.astype(jnp.bfloat16).astype(jnp.float32)

    def unit(values):
        scale = lax.rsqrt(jnp.mean(values * values, axis=0, keepdims=True) + 1e-06)
        return values * scale / math.sqrt(width)

    queries, keys, values = project(wq_ref), project(wk_ref), project(wv_ref)
    eta = rates_ref[...] * live_row(bounds_ref, length)
    rows = iota2((MINI, MINI), 0)
    cols = iota2((MINI, MINI), 1)
    first = iota2((width, 2 * width), 1)
    eye = (first == iota2((width, 2 * width), 0)).astype(jnp.float32)
    low = low_rows(width)
    for h in range(heads):
        part = slice(h * width, (h + 1) * width)
        key_t = unit(keys[part])
        q = unit(queries[part]).T
        gain_t = key_t * eta[h : h + 1]
        kv = jnp.concatenate([-key_t, values[part]], axis=0).T
        pairs = []
        for n in range(blocks):
            span = slice(n * MINI, (n + 1) * MINI)
            gain_n = gain_t[:, span]
            scores = dot(q[span], gain_n)
            left = jnp.concatenate(
                [jnp.where(cols <= rows, scores, 0.0), jnp.where(cols >= rows, scores, 0.0), gain_n], axis=0
            )
            both = dot(left, kv[span])
            q_wide = jnp.concatenate([q[span], jnp.zeros_like(q[span])], axis=1)
            pair = both[2 * MINI :] + eye
            terms_ref[h, n, 0] = both[:MINI] + q_wide
            terms_ref[h, n, 1] = both[MINI : 2 * MINI] + q_wide
            terms_ref[h, n, 2] = pair
            pairs.append(pair)
        ahead, back = pairs[0], pairs[-1]
        for n in range(1, blocks):
            ahead = dot(pairs[n], homog(ahead, low))
            back = dot(pairs[blocks - 1 - n], homog(back, low))
        maps_ref[0, h] = ahead
        maps_ref[1, h] = back


def local_terms(bounds, x, wq, wk, wv, rates_t, heads, width):
    blocks = x.shape[1] // MINI
    whole = pl.BlockSpec(memory_space=VMEM)
    return pl.pallas_call(
        functools.partial(local_kernel, heads, width),
        out_shape=(
            jax.ShapeDtypeStruct((heads, blocks, 3, width, 2 * width), jnp.float32),
            jax.ShapeDtypeStruct((2, heads, width, 2 * width), jnp.float32),
        ),
        in_specs=[pl.BlockSpec(memory_space=pltpu.SMEM)] + [whole] * 5,
        out_specs=(whole, whole),
        compiler_params=pltpu.CompilerParams(vmem_limit_bytes=40 << 20),
        name="local_terms",
    )(bounds, x, wq, wk, wv, rates_t)


def pack(state):
    half = state.shape[0] // 2
    return jnp.concatenate([state[:half], state[half:]], axis=1)


def unpack(packed):
    width = packed.shape[1] // 2
    return jnp.concatenate([packed[:, :width], packed[:, width:]], axis=0)


def prefix_kernel(count, maps_ref, w_ref, out_ref, cur, got, states, got_states, send_sem, recv_sem):
    heads, width = w_ref.shape[0], w_ref.shape[1]
    chips = count // 2
    place = lax.axis_index("seq")
    core = lax.rem(place, 2)
    chip = place // 2
    sign = 1 - 2 * core
    steps = []
    d = 1
    while 2 * d < chips:
        steps.append(d)
        d *= 2
    half = d
    other = place + sign

    def ring(hop):
        return lax.rem(chip + sign * hop + 2 * chips, chips) * 2 + core

    barrier = pltpu.get_barrier_semaphore()
    greet = [other]
    for hop in steps:
        greet += [ring(hop), ring(-hop)]
    greet.append(ring(half))
    for peer in greet:
        pl.semaphore_signal(barrier, inc=1, device_id={"seq": peer}, device_id_type=MESH)
    pl.semaphore_wait(barrier, len(greet))

    def send(index, src, dst, peer):
        return pltpu.make_async_remote_copy(
            src_ref=src,
            dst_ref=dst,
            send_sem=send_sem.at[index],
            recv_sem=recv_sem.at[index],
            device_id={"seq": peer},
            device_id_type=MESH,
        )

    low = low_rows(width)
    eye = (iota2((width, width), 1) == iota2((width, width), 0)).astype(jnp.float32)
    order = chip * (1 - core) + (chips - 1 - chip) * core

    copies = []
    first = send(0, maps_ref.at[1 - core], got.at[0], other)
    first.start()
    copies.append(first)
    first.wait_recv()
    for h in range(heads):
        cur[0, h] = dot(got[0, h], homog(maps_ref[core, h], low))
    for i, hop in enumerate(steps):
        copy = send(i + 1, cur.at[i], got.at[i + 1], ring(hop))
        copy.start()
        copies.append(copy)
        copy.wait_recv()
        keep = order >= hop
        for h in range(heads):
            mine = cur[i, h]
            cur[i + 1, h] = jnp.where(keep, dot(mine, homog(got[i + 1, h], low)), mine)
    last = len(steps)

    def apply(pair, state):
        return dot(pair, jnp.concatenate([state, eye], axis=0))

    for h in range(heads):
        states[0, h] = pack(apply(cur[last, h], w_ref[h]))
    base = last + 1
    copy = send(base, states.at[0], got_states.at[0], ring(half))
    copy.start()
    copies.append(copy)
    copy.wait_recv()
    keep = order >= half
    for h in range(heads):
        full = pack(apply(cur[last, h], unpack(got_states[0, h])))
        states[1, h] = jnp.where(keep, full, states[0, h])
    copy = send(base + 1, states.at[1], got_states.at[1], ring(1))
    copy.start()
    copies.append(copy)
    copy.wait_recv()
    for h in range(heads):
        entry = jnp.where(order >= 1, unpack(got_states[1, h]), w_ref[h])
        out_ref[core, h] = entry
        states[2, h] = pack(apply(maps_ref[core, h], entry))
    copy = send(base + 2, states.at[2], got_states.at[2], other)
    copy.start()
    copies.append(copy)
    copy.wait_recv()
    for h in range(heads):
        out_ref[1 - core, h] = unpack(got_states[2, h])
    for copy in copies:
        copy.wait_send()


def prefix(maps, w_init, count):
    _, heads, width, wide = maps.shape
    rounds = max(1, int(math.log2(count // 2)))
    whole = pl.BlockSpec(memory_space=VMEM)
    return pl.pallas_call(
        functools.partial(prefix_kernel, count),
        out_shape=jax.ShapeDtypeStruct((2, heads, width, width), jnp.float32),
        in_specs=[whole, whole],
        out_specs=whole,
        scratch_shapes=[
            VMEM((rounds, heads, width, wide), jnp.float32),
            VMEM((rounds, heads, width, wide), jnp.float32),
            VMEM((3, heads, width // 2, wide), jnp.float32),
            VMEM((3, heads, width // 2, wide), jnp.float32),
            pltpu.SemaphoreType.DMA((rounds + 3,)),
            pltpu.SemaphoreType.DMA((rounds + 3,)),
        ],
        compiler_params=pltpu.CompilerParams(collective_id=1, has_side_effects=True),
        name="prefix_states",
    )(maps, w_init)


def finish_kernel(heads, width, bounds_ref, terms_ref, entry_ref, gain_ref, out_ref):
    blocks = terms_ref.shape[1]
    length = blocks * MINI
    live = live_row(bounds_ref, length)
    eye = (iota2((width, width), 1) == iota2((width, width), 0)).astype(jnp.float32)

    def norm(values):
        centre = values - jnp.mean(values, axis=0, keepdims=True)
        return centre * lax.rsqrt(jnp.mean(centre * centre, axis=0, keepdims=True) + 1e-05)

    for h in range(heads):
        total = None
        for way in range(2):
            state = entry_ref[way, h]
            rows = [None] * blocks
            order = range(blocks) if way == 0 else range(blocks - 1, -1, -1)
            for n in order:
                left = jnp.concatenate([terms_ref[h, n, way], terms_ref[h, n, 2]], axis=0)
                both = dot(left, jnp.concatenate([state, eye], axis=0))
                rows[n] = both[:MINI]
                state = both[MINI:]
            result = norm(jnp.concatenate(rows, axis=0).T)
            total = result if total is None else total + result
        part = pl.ds(h * width, width)
        out_ref[part, :] = (total * gain_ref[part, :] * live).astype(out_ref.dtype)


def finish(bounds, terms, entry, gain, length):
    heads, _, _, width, _ = terms.shape
    whole = pl.BlockSpec(memory_space=VMEM)
    return pl.pallas_call(
        functools.partial(finish_kernel, heads, width),
        out_shape=jax.ShapeDtypeStruct((heads * width, length), jnp.bfloat16),
        in_specs=[pl.BlockSpec(memory_space=pltpu.SMEM), whole, whole, whole],
        out_specs=whole,
        compiler_params=pltpu.CompilerParams(vmem_limit_bytes=40 << 20),
        name="finish",
    )(bounds, terms, entry, gain)


def on_device(ranks, count, features, w_query, w_key, w_value, rates, scene_bounds, w_init, out_gain):
    length = features.shape[1]
    heads, width = w_init.shape[0], w_init.shape[1]
    piece = gather(features, ranks).reshape(-1, length)
    terms, maps = local_terms(scene_bounds, piece, w_query, w_key, w_value, rates.T, heads, width)
    entry = prefix(maps, w_init, count)
    return finish(scene_bounds, terms, entry, out_gain[:, None], length)


def solution(mesh):
    return jax.shard_map(
        functools.partial(on_device, mesh.shape["head"], mesh.shape["seq"]),
        mesh=mesh,
        in_specs=(
            P("head", "seq"),
            P("head", None),
            P("head", None),
            P("head", None),
            P("seq", "head"),
            P("seq", None),
            P("head", None, None),
            P("head"),
        ),
        out_specs=P("head", "seq"),
        check_vma=False,
    )
```

```python
import functools
import math

import jax
import jax.numpy as jnp
from jax import lax
from jax.experimental import pallas as pl
from jax.experimental.pallas import tpu as pltpu
from jax.sharding import PartitionSpec as P

MINI = 64
MESH = pl.DeviceIdType.MESH
VMEM = pltpu.VMEM
bf16 = jnp.bfloat16


def dot(a, b):
    return jnp.dot(a.astype(bf16), b.astype(bf16), preferred_element_type=jnp.float32)


def split(a):
    high = a.astype(bf16)
    return high, (a - high.astype(jnp.float32)).astype(bf16)


def dot_left(a, b):
    high, rest = split(a)
    return dot(high, b) + dot(rest, b)


def dot_right(a, b):
    high, rest = split(b)
    return dot(a, high) + dot(a, rest)


def dot_both(a, b):
    high, rest = split(a)
    return dot_right(high, b) + dot(rest, b)


def iota2(shape, axis):
    return lax.broadcasted_iota(jnp.int32, shape, axis)


def eye_at(rows, cols, shift):
    return (iota2((rows, cols), 1) == iota2((rows, cols), 0) + shift).astype(jnp.float32)


def stack(upper, lower):
    return jnp.concatenate([upper, lower.astype(upper.dtype)], axis=0)


def pack(state):
    half = state.shape[0] // 2
    return jnp.concatenate([state[:half], state[half:]], axis=1)


def unpack(packed):
    width = packed.shape[1] // 2
    return jnp.concatenate([packed[:, :width], packed[:, width:]], axis=0)


def remote(src, dst, sems, index, peer):
    return pltpu.make_async_remote_copy(
        src_ref=src,
        dst_ref=dst,
        send_sem=sems[0].at[index],
        recv_sem=sems[1].at[index],
        device_id=peer,
        device_id_type=MESH,
    )


def local_terms(heads, width, live, queries, keys, values, rates_ref, terms, maps, maps_low):
    length = queries.shape[1]
    blocks = length // MINI

    def unit(rows):
        scale = lax.rsqrt(jnp.mean(rows * rows, axis=0, keepdims=True) + 1e-06)
        return rows * scale / math.sqrt(width)

    eta = rates_ref[...] * live
    rows = iota2((MINI, MINI), 0)
    cols = iota2((MINI, MINI), 1)
    eye = eye_at(width, 2 * width, 0)
    low = eye_at(width, 2 * width, width)
    for h in range(heads):
        part = slice(h * width, (h + 1) * width)
        key_t = unit(keys[part])
        q = unit(queries[part]).T
        gain_t = key_t * eta[h : h + 1]
        kv = jnp.concatenate([-key_t, values[part]], axis=0).T.astype(bf16)
        pairs = []
        for n in range(blocks):
            span = slice(n * MINI, (n + 1) * MINI)
            gain_n = gain_t[:, span]
            scores = dot(q[span], gain_n)
            left = jnp.concatenate(
                [jnp.where(cols <= rows, scores, 0.0), jnp.where(cols >= rows, scores, 0.0), gain_n], axis=0
            )
            both = dot(left, kv[span])
            q_wide = jnp.concatenate([q[span], jnp.zeros_like(q[span])], axis=1)
            pair = both[2 * MINI :].astype(bf16)
            terms[h, n, 0] = (both[:MINI] + q_wide).astype(bf16)
            terms[h, n, 1] = (both[MINI : 2 * MINI] + q_wide).astype(bf16)
            terms[h, n, 2] = pair
            pairs.append(pair)
        for way in range(2):
            order = pairs if way == 0 else pairs[::-1]
            total = order[0].astype(jnp.float32) + eye
            for pair in order[1:]:
                total = total + dot(pair, stack(total, low))
            maps[way, h] = total
            maps_low[way, h] = total.astype(bf16)


def prefix(count, maps, maps_low, w_ref, entry, cur, out_maps, got, states, got_states, sems, peers):
    heads, width = w_ref.shape[0], w_ref.shape[1]
    core, order, steps, far, other, ring = peers
    low = eye_at(width, 2 * width, width)
    eye = eye_at(width, width, 0)
    copies = []

    def move(index, src, dst, peer):
        copy = remote(src, dst, sems, index, {"seq": peer})
        copy.start()
        copies.append(copy)
        return copy

    move(0, maps_low.at[1 - core], got.at[0], other).wait_recv()
    for h in range(heads):
        total = dot_right(got[0, h], stack(maps[core, h], low))
        cur[h] = total
        out_maps[0, h] = total.astype(bf16)
    for i, hop in enumerate(steps):
        move(i + 1, out_maps.at[i], got.at[i + 1], ring(hop)).wait_recv()
        keep = order >= hop
        for h in range(heads):
            mine = cur[h]
            total = jnp.where(keep, dot_left(mine, stack(got[i + 1, h], low)), mine)
            cur[h] = total
            out_maps[i + 1, h] = total.astype(bf16)
    base = len(steps)
    for h in range(heads):
        states[0, h] = pack(dot_both(cur[h], stack(w_ref[h], eye))).astype(bf16)
    ahead = move(base + 2, states.at[0], got_states.at[0], ring(far))
    move(base + 1, out_maps.at[base], got.at[base + 1], ring(1)).wait_recv()
    ahead.wait_recv()
    for h in range(heads):
        start = w_ref[h]
        before = jnp.where(order >= far, unpack(got_states[0, h].astype(jnp.float32)), start)
        state = jnp.where(order >= 1, dot_right(got[base + 1, h], stack(before, eye)), start)
        entry[core, h] = state
        states[1, h] = pack(dot_both(maps[core, h], stack(state, eye))).astype(bf16)
    move(base + 3, states.at[1], got_states.at[1], other).wait_recv()
    for h in range(heads):
        entry[1 - core, h] = unpack(got_states[1, h].astype(jnp.float32))
    for copy in copies:
        copy.wait_send()


def finish(heads, width, live, terms, entry, gain_ref, out_ref):
    blocks = terms.shape[1]
    eye = eye_at(width, width, 0)

    def norm(values):
        centre = values - jnp.mean(values, axis=0, keepdims=True)
        return centre * lax.rsqrt(jnp.mean(centre * centre, axis=0, keepdims=True) + 1e-05)

    rows = {}
    states = {(h, way): entry[way, h] for h in range(heads) for way in range(2)}
    for step in range(blocks):
        for h in range(heads):
            for way in range(2):
                n = step if way == 0 else blocks - 1 - step
                state = states[h, way]
                left = jnp.concatenate([terms[h, n, way], terms[h, n, 2]], axis=0)
                both = dot(left, stack(state, eye))
                rows[h, way, n] = both[:MINI]
                states[h, way] = state + both[MINI:]
    for h in range(heads):
        total = 0.0
        for way in range(2):
            total = total + norm(jnp.concatenate([rows[h, way, n] for n in range(blocks)], axis=0).T)
        part = pl.ds(h * width, width)
        out_ref[part, :] = (total * gain_ref[part, :] * live).astype(out_ref.dtype)


def kernel(
    ranks, count, bounds_ref, x_ref, wq_ref, wk_ref, wv_ref, rates_ref, w_ref, gain_ref, out_ref,
    gathered, weights, terms, maps, maps_low, entry, cur, out_maps, got, states, got_states,
    local_sem, gather_send, gather_recv, send_sem, recv_sem,
):
    heads, width = w_ref.shape[0], w_ref.shape[1]
    length = x_ref.shape[1]
    me = lax.axis_index("head")
    place = lax.axis_index("seq")
    chips = count // 2
    core = lax.rem(place, 2)
    chip = place // 2
    sign = 1 - 2 * core
    steps = []
    hop = 1
    while 2 * hop < chips:
        steps.append(hop)
        hop *= 2
    far = hop + 1
    other = place + sign
    order = chip * (1 - core) + (chips - 1 - chip) * core

    def ring(hops):
        return lax.rem(chip + sign * hops + 2 * chips, chips) * 2 + core

    barrier = pltpu.get_barrier_semaphore()
    greet = [{"seq": other}, {"seq": ring(far)}, {"seq": ring(-far)}]
    for hops in steps:
        greet += [{"seq": ring(hops)}, {"seq": ring(-hops)}]
    for off in range(1, ranks):
        greet.append({"head": lax.rem(me + off, ranks)})
    for peer in greet:
        pl.semaphore_signal(barrier, inc=1, device_id=peer, device_id_type=MESH)
    loads = [pltpu.make_async_copy(x_ref, gathered.at[me], local_sem.at[0])]
    for i, ref in enumerate((wq_ref, wk_ref, wv_ref)):
        loads.append(pltpu.make_async_copy(ref, weights.at[i], local_sem.at[i + 1]))
    for load in loads:
        load.start()
    pl.semaphore_wait(barrier, len(greet))

    sems = (gather_send, gather_recv)
    for off in range(1, ranks):
        remote(x_ref, gathered.at[me], sems, off, {"head": lax.rem(me + off, ranks)}).start()
    for load in loads:
        load.wait()
    for off in range(1, ranks):
        source = lax.rem(me - off + ranks, ranks)
        remote(x_ref, gathered.at[source], sems, off, {"head": source}).wait_recv()
    piece = gathered[...].reshape(-1, length)
    projected = []
    for i in range(3):
        total = jnp.dot(weights[i], piece, preferred_element_type=jnp.float32)
        projected.append(total.astype(bf16).astype(jnp.float32))
    slots = iota2((1, length), 1)
    live = ((slots >= bounds_ref[0, 0]) & (slots < bounds_ref[0, 1])).astype(jnp.float32)
    local_terms(heads, width, live, *projected, rates_ref, terms, maps, maps_low)
    peers = (core, order, steps, far, other, ring)
    prefix(count, maps, maps_low, w_ref, entry, cur, out_maps, got, states, got_states, (send_sem, recv_sem), peers)
    finish(heads, width, live, terms, entry, gain_ref, out_ref)
    for off in range(1, ranks):
        remote(x_ref, gathered.at[me], sems, off, {"head": lax.rem(me + off, ranks)}).wait_send()


def on_device(ranks, count, features, w_query, w_key, w_value, rates, scene_bounds, w_init, out_gain):
    length = features.shape[1]
    heads, width = w_init.shape[0], w_init.shape[1]
    wide = 2 * width
    blocks = length // MINI
    rounds = max(1, int(math.log2(count // 2)))
    here = pl.BlockSpec(memory_space=VMEM)
    away = pl.BlockSpec(memory_space=pl.ANY)
    return pl.pallas_call(
        functools.partial(kernel, ranks, count),
        out_shape=jax.ShapeDtypeStruct((heads * width, length), bf16),
        in_specs=[pl.BlockSpec(memory_space=pltpu.SMEM)] + [away] * 4 + [here] * 3,
        out_specs=here,
        scratch_shapes=[
            VMEM((ranks,) + features.shape, bf16),
            VMEM((3,) + w_query.shape, bf16),
            VMEM((heads, blocks, 3, width, wide), bf16),
            VMEM((2, heads, width, wide), jnp.float32),
            VMEM((2, heads, width, wide), bf16),
            VMEM((2, heads, width, width), jnp.float32),
            VMEM((heads, width, wide), jnp.float32),
            VMEM((rounds, heads, width, wide), bf16),
            VMEM((rounds + 1, heads, width, wide), bf16),
            VMEM((2, heads, width // 2, wide), bf16),
            VMEM((2, heads, width // 2, wide), bf16),
            pltpu.SemaphoreType.DMA((4,)),
            pltpu.SemaphoreType.DMA((ranks,)),
            pltpu.SemaphoreType.DMA((ranks,)),
            pltpu.SemaphoreType.DMA((rounds + 3,)),
            pltpu.SemaphoreType.DMA((rounds + 3,)),
        ],
        compiler_params=pltpu.CompilerParams(
            collective_id=0, has_side_effects=True, vmem_limit_bytes=58 << 20
        ),
        name="ttt_layer",
    )(scene_bounds, features, w_query, w_key, w_value, rates.T, w_init, out_gain[:, None])


def solution(mesh):
    return jax.shard_map(
        functools.partial(on_device, mesh.shape["head"], mesh.shape["seq"]),
        mesh=mesh,
        in_specs=(
            P("head", "seq"),
            P("head", None),
            P("head", None),
            P("head", None),
            P("seq", "head"),
            P("seq", None),
            P("head", None, None),
            P("head"),
        ),
        out_specs=P("head", "seq"),
        check_vma=False,
    )
```

```python
import functools
import math

import jax
import jax.numpy as jnp
from jax import lax
from jax.experimental import pallas as pl
from jax.experimental.pallas import tpu as pltpu
from jax.sharding import PartitionSpec as P

MINI = 64
MESH = pl.DeviceIdType.MESH
VMEM = pltpu.VMEM
bf16 = jnp.bfloat16


def dot(a, b):
    return jnp.dot(a.astype(bf16), b.astype(bf16), preferred_element_type=jnp.float32)


def split(a):
    high = a.astype(bf16)
    return high, (a - high.astype(jnp.float32)).astype(bf16)


def dot_left(a, b):
    high, rest = split(a)
    return dot(high, b) + dot(rest, b)


def dot_right(a, b):
    high, rest = split(b)
    return dot(a, high) + dot(a, rest)


def dot_both(a, b):
    high, rest = split(a)
    return dot_right(high, b) + dot(rest, b)


def iota2(shape, axis):
    return lax.broadcasted_iota(jnp.int32, shape, axis)


def eye_at(rows, cols, shift):
    return (iota2((rows, cols), 1) == iota2((rows, cols), 0) + shift).astype(jnp.float32)


def stack(upper, lower):
    return jnp.concatenate([upper, lower.astype(upper.dtype)], axis=0)


def pack(state):
    half = state.shape[0] // 2
    return jnp.concatenate([state[:half], state[half:]], axis=1)


def unpack(packed):
    width = packed.shape[1] // 2
    return jnp.concatenate([packed[:, :width], packed[:, width:]], axis=0)


def remote(src, dst, sems, index, peer):
    return pltpu.make_async_remote_copy(
        src_ref=src,
        dst_ref=dst,
        send_sem=sems[0].at[index],
        recv_sem=sems[1].at[index],
        device_id=peer,
        device_id_type=MESH,
    )


def spread(side, me, x_ref, gathered, sems):
    own_x, own_y = lax.rem(me, side), me // side
    half_rows = x_ref.shape[0] // 2
    sent = []

    def wrap(place):
        return lax.rem(place + 2 * side, side)

    def index(half, u, w):
        return wrap(w) * side + wrap(u) if half == 0 else wrap(u) * side + wrap(w)

    def rows(half, piece):
        if piece is None:
            return pl.ds(half * half_rows, half_rows)
        return pl.ds(half * half_rows + piece * (half_rows // 2), half_rows // 2)

    def slot(half, u, w, piece=None):
        return gathered.at[index(half, u, w), rows(half, piece)]

    def place(half):
        return (own_x, own_y) if half == 0 else (own_y, own_x)

    def send(half, number, source, target, peer):
        copy = remote(source, target, sems, 20 * half + number, {"head": peer})
        copy.start()
        sent.append(copy)

    def arrive(half, number, target):
        remote(target, target, sems, 20 * half + number, {"head": index(half, *place(half))}).wait_recv()

    def along(half, axis, hop):
        u, w = place(half)
        return index(half, u + hop, w) if axis == 0 else index(half, u, w + hop)

    def open_stream(half, axis, base, u, w, source):
        for number, hop in ((0, 1), (1, -1)):
            send(half, base + number, source, slot(half, u, w), along(half, axis, hop))

    def relay(half, axis, base, u, w):
        for number, hop in ((0, 1), (1, -1)):
            au, aw = (u - hop, w) if axis == 0 else (u, w - hop)
            arrive(half, base + number, slot(half, au, aw))
            block = slot(half, au, aw, number)
            send(half, base + 2 + number, block, block, along(half, axis, hop))
            if axis == 0:
                whole = slot(half, au, aw)
                open_stream(half, 1, 8 + 4 * number, au, aw, whole)

    def close(half, axis, base, u, w):
        au, aw = (u + 2, w) if axis == 0 else (u, w + 2)
        for number in range(2):
            arrive(half, base + 2 + number, slot(half, au, aw, number))
        if axis == 0:
            open_stream(half, 1, 16, au, aw, slot(half, au, aw))

    def own(half):
        return x_ref.at[rows(half, None)]

    halves = range(2)
    for half in halves:
        open_stream(half, 0, 0, *place(half), own(half))
    for half in halves:
        open_stream(half, 1, 4, *place(half), own(half))
    for half in halves:
        relay(half, 0, 0, *place(half))
    for half in halves:
        close(half, 0, 0, *place(half))
    shifts = (0, -1, 1, 2)
    for step in range(5):
        for half in halves:
            u, w = place(half)
            if step < 4:
                relay(half, 1, 4 + 4 * step, u + shifts[step], w)
            if step > 0:
                close(half, 1, 4 * step, u + shifts[step - 1], w)
    return sent


def local_terms(heads, width, live, queries, keys, values, rates_ref, terms, maps, maps_low):
    length = queries.shape[1]
    blocks = length // MINI

    def unit(rows):
        scale = lax.rsqrt(jnp.mean(rows * rows, axis=0, keepdims=True) + 1e-06)
        return rows * scale / math.sqrt(width)

    eta = rates_ref[...] * live
    rows = iota2((MINI, MINI), 0)
    cols = iota2((MINI, MINI), 1)
    eye = eye_at(width, 2 * width, 0)
    low = eye_at(width, 2 * width, width)
    for h in range(heads):
        part = slice(h * width, (h + 1) * width)
        key_t = unit(keys[part])
        q = unit(queries[part]).T
        gain_t = key_t * eta[h : h + 1]
        kv = jnp.concatenate([-key_t, values[part]], axis=0).T.astype(bf16)
        pairs = []
        for n in range(blocks):
            span = slice(n * MINI, (n + 1) * MINI)
            gain_n = gain_t[:, span]
            scores = dot(q[span], gain_n)
            left = jnp.concatenate(
                [jnp.where(cols <= rows, scores, 0.0), jnp.where(cols >= rows, scores, 0.0), gain_n], axis=0
            )
            both = dot(left, kv[span])
            q_wide = jnp.concatenate([q[span], jnp.zeros_like(q[span])], axis=1)
            pair = both[2 * MINI :]
            terms[h, n, 0] = both[:MINI] + q_wide
            terms[h, n, 1] = both[MINI : 2 * MINI] + q_wide
            terms[h, n, 2] = pair
            pairs.append(pair)
        for way in range(2):
            order = pairs if way == 0 else pairs[::-1]
            total = order[0].astype(jnp.float32) + eye
            for pair in order[1:]:
                total = total + dot_left(pair, stack(total, low))
            maps[way, h] = total
            maps_low[way, h] = total.astype(bf16)


def prefix(count, maps, maps_low, w_ref, entry, cur, out_maps, got, states, got_states, sems, peers):
    heads, width = w_ref.shape[0], w_ref.shape[1]
    core, order, steps, far, other, ring = peers
    low = eye_at(width, 2 * width, width)
    eye = eye_at(width, width, 0)
    copies = []

    def move(index, src, dst, peer):
        copy = remote(src, dst, sems, index, {"seq": peer})
        copy.start()
        copies.append(copy)
        return copy

    move(0, maps_low.at[1 - core], got.at[0], other).wait_recv()
    for h in range(heads):
        total = dot_right(got[0, h], stack(maps[core, h], low))
        cur[h] = total
        out_maps[0, h] = total.astype(bf16)
    for i, hop in enumerate(steps):
        move(i + 1, out_maps.at[i], got.at[i + 1], ring(hop)).wait_recv()
        keep = order >= hop
        for h in range(heads):
            mine = cur[h]
            total = jnp.where(keep, dot_left(mine, stack(got[i + 1, h], low)), mine)
            cur[h] = total
            out_maps[i + 1, h] = total.astype(bf16)
    base = len(steps)
    for h in range(heads):
        states[0, h] = pack(dot_both(cur[h], stack(w_ref[h], eye))).astype(bf16)
    ahead = move(base + 2, states.at[0], got_states.at[0], ring(far))
    move(base + 1, out_maps.at[base], got.at[base + 1], ring(1)).wait_recv()
    ahead.wait_recv()
    for h in range(heads):
        start = w_ref[h]
        before = jnp.where(order >= far, unpack(got_states[0, h].astype(jnp.float32)), start)
        state = jnp.where(order >= 1, dot_right(got[base + 1, h], stack(before, eye)), start)
        entry[core, h] = state
        states[1, h] = pack(dot_both(maps[core, h], stack(state, eye))).astype(bf16)
    move(base + 3, states.at[1], got_states.at[1], other).wait_recv()
    for h in range(heads):
        entry[1 - core, h] = unpack(got_states[1, h].astype(jnp.float32))
    for copy in copies:
        copy.wait_send()


def finish(heads, width, live, terms, entry, gain_ref, out_ref):
    blocks = terms.shape[1]
    eye = eye_at(width, width, 0)

    def norm(values):
        centre = values - jnp.mean(values, axis=0, keepdims=True)
        return centre * lax.rsqrt(jnp.mean(centre * centre, axis=0, keepdims=True) + 1e-05)

    gain = jnp.broadcast_to(gain_ref[...], (8, heads * width)).T[:, :1]
    rows = {}
    states = {(h, way): entry[way, h] for h in range(heads) for way in range(2)}
    for step in range(blocks):
        for h in range(heads):
            for way in range(2):
                n = step if way == 0 else blocks - 1 - step
                state = states[h, way]
                left = jnp.concatenate([terms[h, n, way], terms[h, n, 2]], axis=0)
                both = dot_both(left, stack(state, eye))
                rows[h, way, n] = both[:MINI]
                states[h, way] = state + both[MINI:]
    for h in range(heads):
        total = 0.0
        for way in range(2):
            total = total + norm(jnp.concatenate([rows[h, way, n] for n in range(blocks)], axis=0).T)
        part = pl.ds(h * width, width)
        out_ref[part, :] = (total * gain[h * width : (h + 1) * width] * live).astype(out_ref.dtype)


def kernel(
    ranks, count, bounds_ref, x_ref, wq_ref, wk_ref, wv_ref, rates_ref, w_ref, gain_ref, out_ref,
    gathered, weights, terms, maps, maps_low, entry, cur, out_maps, got, states, got_states,
    local_sem, gather_send, gather_recv, send_sem, recv_sem,
):
    heads, width = w_ref.shape[0], w_ref.shape[1]
    length = x_ref.shape[1]
    me = lax.axis_index("head")
    place = lax.axis_index("seq")
    chips = count // 2
    core = lax.rem(place, 2)
    chip = place // 2
    sign = 1 - 2 * core
    steps = []
    hop = 1
    while 2 * hop < chips:
        steps.append(hop)
        hop *= 2
    far = hop + 1
    other = place + sign
    order = chip * (1 - core) + (chips - 1 - chip) * core

    def ring(hops):
        return lax.rem(chip + sign * hops + 2 * chips, chips) * 2 + core

    barrier = pltpu.get_barrier_semaphore()
    greet = [{"seq": other}, {"seq": ring(far)}, {"seq": ring(-far)}]
    for hops in steps:
        greet += [{"seq": ring(hops)}, {"seq": ring(-hops)}]
    side = math.isqrt(ranks)
    own_x, own_y = lax.rem(me, side), me // side
    if side > 1:
        for hop in (1, side - 1):
            greet.append({"head": own_y * side + lax.rem(own_x + hop, side)})
            greet.append({"head": lax.rem(own_y + hop, side) * side + own_x})
    for peer in greet:
        pl.semaphore_signal(barrier, inc=1, device_id=peer, device_id_type=MESH)
    loads = [pltpu.make_async_copy(x_ref, gathered.at[me], local_sem.at[0])]
    for i, ref in enumerate((wq_ref, wk_ref, wv_ref)):
        loads.append(pltpu.make_async_copy(ref, weights.at[i], local_sem.at[i + 1]))
    for load in loads:
        load.start()
    pl.semaphore_wait(barrier, len(greet))

    sent = []
    if side > 1:
        sent = spread(side, me, x_ref, gathered, (gather_send, gather_recv))
    for load in loads:
        load.wait()
    piece = gathered[...].reshape(-1, length)
    projected = []
    for i in range(3):
        total = jnp.dot(weights[i], piece, preferred_element_type=jnp.float32)
        projected.append(total.astype(bf16).astype(jnp.float32))
    slots = iota2((1, length), 1)
    live = ((slots >= bounds_ref[0, 0]) & (slots < bounds_ref[0, 1])).astype(jnp.float32)
    local_terms(heads, width, live, *projected, rates_ref, terms, maps, maps_low)
    peers = (core, order, steps, far, other, ring)
    prefix(count, maps, maps_low, w_ref, entry, cur, out_maps, got, states, got_states, (send_sem, recv_sem), peers)
    finish(heads, width, live, terms, entry, gain_ref, out_ref)
    for copy in sent:
        copy.wait_send()


def on_device(ranks, count, features, w_query, w_key, w_value, rates, scene_bounds, w_init, out_gain):
    length = features.shape[1]
    heads, width = w_init.shape[0], w_init.shape[1]
    wide = 2 * width
    blocks = length // MINI
    rounds = max(1, int(math.log2(count // 2)))
    here = pl.BlockSpec(memory_space=VMEM)
    away = pl.BlockSpec(memory_space=pl.ANY)
    return pl.pallas_call(
        functools.partial(kernel, ranks, count),
        out_shape=jax.ShapeDtypeStruct((heads * width, length), bf16),
        in_specs=[pl.BlockSpec(memory_space=pltpu.SMEM)] + [away] * 4 + [here] * 3,
        out_specs=here,
        scratch_shapes=[
            VMEM((ranks,) + features.shape, bf16),
            VMEM((3,) + w_query.shape, bf16),
            VMEM((heads, blocks, 3, width, wide), jnp.float32),
            VMEM((2, heads, width, wide), jnp.float32),
            VMEM((2, heads, width, wide), bf16),
            VMEM((2, heads, width, width), jnp.float32),
            VMEM((heads, width, wide), jnp.float32),
            VMEM((rounds, heads, width, wide), bf16),
            VMEM((rounds + 1, heads, width, wide), bf16),
            VMEM((2, heads, width // 2, wide), bf16),
            VMEM((2, heads, width // 2, wide), bf16),
            pltpu.SemaphoreType.DMA((4,)),
            pltpu.SemaphoreType.DMA((40,)),
            pltpu.SemaphoreType.DMA((40,)),
            pltpu.SemaphoreType.DMA((rounds + 3,)),
            pltpu.SemaphoreType.DMA((rounds + 3,)),
        ],
        compiler_params=pltpu.CompilerParams(
            collective_id=0, has_side_effects=True, vmem_limit_bytes=58 << 20
        ),
        name="ttt_layer",
    )(scene_bounds, features, w_query, w_key, w_value, rates.T, w_init, out_gain[None, :])


def solution(mesh):
    return jax.shard_map(
        functools.partial(on_device, mesh.shape["head"], mesh.shape["seq"]),
        mesh=mesh,
        in_specs=(
            P("head", "seq"),
            P("head", None),
            P("head", None),
            P("head", None),
            P("seq", "head"),
            P("seq", None),
            P("head", None, None),
            P("head"),
        ),
        out_specs=P("head", "seq"),
        check_vma=False,
    )
```

```python
import functools
import math

import jax
import jax.numpy as jnp
from jax import lax
from jax.experimental import pallas as pl
from jax.experimental.pallas import tpu as pltpu
from jax.sharding import PartitionSpec as P

MINI = 64
MESH = pl.DeviceIdType.MESH
VMEM = pltpu.VMEM
bf16 = jnp.bfloat16


def dot(a, b):
    return jnp.dot(a.astype(bf16), b.astype(bf16), preferred_element_type=jnp.float32)


def split(a):
    high = a.astype(bf16)
    return high, (a - high.astype(jnp.float32)).astype(bf16)


def dot_left(a, b):
    high, rest = split(a)
    return dot(high, b) + dot(rest, b)


def dot_right(a, b):
    high, rest = split(b)
    return dot(a, high) + dot(a, rest)


def dot_both(a, b):
    high, rest = split(a)
    return dot_right(high, b) + dot(rest, b)


def iota2(shape, axis):
    return lax.broadcasted_iota(jnp.int32, shape, axis)


def eye_at(rows, cols, shift):
    return (iota2((rows, cols), 1) == iota2((rows, cols), 0) + shift).astype(jnp.float32)


def stack(upper, lower):
    return jnp.concatenate([upper, lower.astype(upper.dtype)], axis=0)


def pack(state):
    half = state.shape[0] // 2
    return jnp.concatenate([state[:half], state[half:]], axis=1)


def unpack(packed):
    width = packed.shape[1] // 2
    return jnp.concatenate([packed[:, :width], packed[:, width:]], axis=0)


def remote(src, dst, sems, index, peer):
    return pltpu.make_async_remote_copy(
        src_ref=src,
        dst_ref=dst,
        send_sem=sems[0].at[index],
        recv_sem=sems[1].at[index],
        device_id=peer,
        device_id_type=MESH,
    )


def spread(side, me, x_ref, gathered, sems):
    own_x, own_y = lax.rem(me, side), me // side
    half_rows = x_ref.shape[0] // 2
    sent = []

    def wrap(place):
        return lax.rem(place + 2 * side, side)

    def index(half, u, w):
        return wrap(w) * side + wrap(u) if half == 0 else wrap(u) * side + wrap(w)

    def rows(half, piece):
        if piece is None:
            return pl.ds(half * half_rows, half_rows)
        return pl.ds(half * half_rows + piece * (half_rows // 2), half_rows // 2)

    def slot(half, u, w, piece=None):
        return gathered.at[index(half, u, w), rows(half, piece)]

    def place(half):
        return (own_x, own_y) if half == 0 else (own_y, own_x)

    def send(half, number, source, target, peer):
        copy = remote(source, target, sems, 20 * half + number, {"head": peer})
        copy.start()
        sent.append(copy)

    def arrive(half, number, target):
        remote(target, target, sems, 20 * half + number, {"head": index(half, *place(half))}).wait_recv()

    def along(half, axis, hop):
        u, w = place(half)
        return index(half, u + hop, w) if axis == 0 else index(half, u, w + hop)

    def open_stream(half, axis, base, u, w, source):
        for number, hop in ((0, 1), (1, -1)):
            send(half, base + number, source, slot(half, u, w), along(half, axis, hop))

    def relay(half, axis, base, u, w):
        for number, hop in ((0, 1), (1, -1)):
            au, aw = (u - hop, w) if axis == 0 else (u, w - hop)
            arrive(half, base + number, slot(half, au, aw))
            block = slot(half, au, aw, number)
            send(half, base + 2 + number, block, block, along(half, axis, hop))
            if axis == 0:
                whole = slot(half, au, aw)
                open_stream(half, 1, 8 + 4 * number, au, aw, whole)

    def close(half, axis, base, u, w):
        au, aw = (u + 2, w) if axis == 0 else (u, w + 2)
        for number in range(2):
            arrive(half, base + 2 + number, slot(half, au, aw, number))
        if axis == 0:
            open_stream(half, 1, 16, au, aw, slot(half, au, aw))

    def own(half):
        return x_ref.at[rows(half, None)]

    halves = range(2)
    for half in halves:
        open_stream(half, 0, 0, *place(half), own(half))
    for half in halves:
        open_stream(half, 1, 4, *place(half), own(half))
    for half in halves:
        relay(half, 0, 0, *place(half))
    for half in halves:
        close(half, 0, 0, *place(half))
    shifts = (0, -1, 1, 2)
    for step in range(5):
        for half in halves:
            u, w = place(half)
            if step < 4:
                relay(half, 1, 4 + 4 * step, u + shifts[step], w)
            if step > 0:
                close(half, 1, 4 * step, u + shifts[step - 1], w)
    return sent


def unit(rows):
    scale = lax.rsqrt(jnp.mean(rows * rows, axis=0, keepdims=True) + 1e-06)
    return rows * scale / math.sqrt(rows.shape[0])


def local_maps(heads, width, live, keys, values, rates_ref, terms, maps, maps_low):
    length = keys.shape[1]
    blocks = length // MINI
    eta = rates_ref[...] * live
    eye = eye_at(width, 2 * width, 0)
    low = eye_at(width, 2 * width, width)
    kept = []
    for h in range(heads):
        part = slice(h * width, (h + 1) * width)
        key_t = unit(keys[part])
        gain_t = (key_t * eta[h : h + 1]).astype(bf16)
        kv = jnp.concatenate([-key_t, values[part]], axis=0).T.astype(bf16)
        kept.append((gain_t, kv))
        pairs = []
        for n in range(blocks):
            span = slice(n * MINI, (n + 1) * MINI)
            pair = dot(gain_t[:, span], kv[span])
            terms[h, n, 2] = pair
            pairs.append(pair)
        for way in range(2):
            order = pairs if way == 0 else pairs[::-1]
            total = order[0] + eye
            for pair in order[1:]:
                total = total + dot_left(pair, stack(total, low))
            maps[way, h] = total
            maps_low[way, h] = total.astype(bf16)
    return kept


def local_outputs(h, query_t, gain_t, kv, terms):
    blocks = query_t.shape[1] // MINI
    rows = iota2((MINI, MINI), 0)
    cols = iota2((MINI, MINI), 1)
    q = unit(query_t).T
    for n in range(blocks):
        span = slice(n * MINI, (n + 1) * MINI)
        scores = dot(q[span], gain_t[:, span])
        left = jnp.concatenate([jnp.where(cols <= rows, scores, 0.0), jnp.where(cols >= rows, scores, 0.0)], axis=0)
        both = dot(left, kv[span])
        q_wide = jnp.concatenate([q[span], jnp.zeros_like(q[span])], axis=1)
        terms[h, n, 0] = both[:MINI] + q_wide
        terms[h, n, 1] = both[MINI:] + q_wide


def prefix(count, maps, maps_low, w_ref, entry, cur, out_maps, got, states, got_states, sems, peers, fills):
    heads, width = w_ref.shape[0], w_ref.shape[1]
    core, order, steps, far, other, ring = peers
    low = eye_at(width, 2 * width, width)
    eye = eye_at(width, width, 0)
    copies = []

    def move(index, src, dst, peer):
        copy = remote(src, dst, sems, index, {"seq": peer})
        copy.start()
        copies.append(copy)
        return copy

    def fill():
        if fills:
            fills.pop(0)()

    first = move(0, maps_low.at[1 - core], got.at[0], other)
    fill()
    first.wait_recv()
    for h in range(heads):
        total = dot_right(got[0, h], stack(maps[core, h], low))
        cur[h] = total
        out_maps[0, h] = total.astype(bf16)
    for i, hop in enumerate(steps):
        copy = move(i + 1, out_maps.at[i], got.at[i + 1], ring(hop))
        fill()
        copy.wait_recv()
        keep = order >= hop
        for h in range(heads):
            mine = cur[h]
            total = jnp.where(keep, dot_left(mine, stack(got[i + 1, h], low)), mine)
            cur[h] = total
            out_maps[i + 1, h] = total.astype(bf16)
    base = len(steps)
    for h in range(heads):
        states[0, h] = pack(dot_both(cur[h], stack(w_ref[h], eye))).astype(bf16)
    ahead = move(base + 2, states.at[0], got_states.at[0], ring(far))
    near = move(base + 1, out_maps.at[base], got.at[base + 1], ring(1))
    while fills:
        fill()
    near.wait_recv()
    ahead.wait_recv()
    for h in range(heads):
        start = w_ref[h]
        before = jnp.where(order >= far, unpack(got_states[0, h].astype(jnp.float32)), start)
        state = jnp.where(order >= 1, dot_right(got[base + 1, h], stack(before, eye)), start)
        entry[core, h] = state
        states[1, h] = pack(dot_both(maps[core, h], stack(state, eye))).astype(bf16)
    move(base + 3, states.at[1], got_states.at[1], other).wait_recv()
    for h in range(heads):
        entry[1 - core, h] = unpack(got_states[1, h].astype(jnp.float32))
    for copy in copies:
        copy.wait_send()


def finish(heads, width, live, terms, entry, gain_ref, out_ref):
    blocks = terms.shape[1]
    eye = eye_at(width, width, 0)

    def norm(values):
        centre = values - jnp.mean(values, axis=0, keepdims=True)
        return centre * lax.rsqrt(jnp.mean(centre * centre, axis=0, keepdims=True) + 1e-05)

    gain = jnp.broadcast_to(gain_ref[...], (8, heads * width)).T[:, :1]
    rows = {}
    states = {(h, way): entry[way, h] for h in range(heads) for way in range(2)}
    for step in range(blocks):
        for h in range(heads):
            for way in range(2):
                n = step if way == 0 else blocks - 1 - step
                state = states[h, way]
                left = jnp.concatenate([terms[h, n, way], terms[h, n, 2]], axis=0)
                both = dot_both(left, stack(state, eye))
                rows[h, way, n] = both[:MINI]
                states[h, way] = state + both[MINI:]
    for h in range(heads):
        total = 0.0
        for way in range(2):
            total = total + norm(jnp.concatenate([rows[h, way, n] for n in range(blocks)], axis=0).T)
        part = pl.ds(h * width, width)
        out_ref[part, :] = (total * gain[h * width : (h + 1) * width] * live).astype(out_ref.dtype)


def kernel(
    ranks, count, bounds_ref, x_ref, wq_ref, wk_ref, wv_ref, rates_ref, w_ref, gain_ref, out_ref,
    gathered, weights, queries, terms, maps, maps_low, entry, cur, out_maps, got, states, got_states,
    local_sem, gather_send, gather_recv, send_sem, recv_sem,
):
    heads, width = w_ref.shape[0], w_ref.shape[1]
    length = x_ref.shape[1]
    me = lax.axis_index("head")
    place = lax.axis_index("seq")
    chips = count // 2
    core = lax.rem(place, 2)
    chip = place // 2
    sign = 1 - 2 * core
    steps = []
    hop = 1
    while 2 * hop < chips:
        steps.append(hop)
        hop *= 2
    far = hop + 1
    other = place + sign
    order = chip * (1 - core) + (chips - 1 - chip) * core

    def ring(hops):
        return lax.rem(chip + sign * hops + 2 * chips, chips) * 2 + core

    barrier = pltpu.get_barrier_semaphore()
    greet = [{"seq": other}]
    for hops in steps:
        greet += [{"seq": ring(hops)}, {"seq": ring(-hops)}]
    side = math.isqrt(ranks)
    own_x, own_y = lax.rem(me, side), me // side
    if side > 1:
        for hop in (1, side - 1):
            greet.append({"head": own_y * side + lax.rem(own_x + hop, side)})
            greet.append({"head": lax.rem(own_y + hop, side) * side + own_x})
    for peer in greet:
        pl.semaphore_signal(barrier, inc=1, device_id=peer, device_id_type=MESH)
    loads = [pltpu.make_async_copy(x_ref, gathered.at[me], local_sem.at[0])]
    for i, ref in enumerate((wq_ref, wk_ref, wv_ref)):
        loads.append(pltpu.make_async_copy(ref, weights.at[i], local_sem.at[i + 1]))
    for load in loads:
        load.start()
    pl.semaphore_wait(barrier, len(greet))

    sent = []
    if side > 1:
        sent = spread(side, me, x_ref, gathered, (gather_send, gather_recv))
    for load in loads:
        load.wait()
    piece = gathered[...].reshape(-1, length)

    def project(i):
        total = jnp.dot(weights[i], piece, preferred_element_type=jnp.float32)
        return total.astype(bf16).astype(jnp.float32)

    slots = iota2((1, length), 1)
    live = ((slots >= bounds_ref[0, 0]) & (slots < bounds_ref[0, 1])).astype(jnp.float32)
    kept = local_maps(heads, width, live, project(1), project(2), rates_ref, terms, maps, maps_low)

    def query_fill():
        queries[...] = jnp.dot(weights[0], gathered[...].reshape(-1, length), preferred_element_type=jnp.float32).astype(bf16)

    def output_fill(h):
        local_outputs(h, queries[pl.ds(h * width, width), :].astype(jnp.float32), *kept[h], terms)

    fills = [query_fill] + [functools.partial(output_fill, h) for h in range(heads)]
    peers = (core, order, steps, far, other, ring)
    prefix(count, maps, maps_low, w_ref, entry, cur, out_maps, got, states, got_states, (send_sem, recv_sem), peers, fills)
    finish(heads, width, live, terms, entry, gain_ref, out_ref)
    for copy in sent:
        copy.wait_send()


def on_device(ranks, count, features, w_query, w_key, w_value, rates, scene_bounds, w_init, out_gain):
    length = features.shape[1]
    heads, width = w_init.shape[0], w_init.shape[1]
    wide = 2 * width
    blocks = length // MINI
    rounds = max(1, int(math.log2(count // 2)))
    here = pl.BlockSpec(memory_space=VMEM)
    away = pl.BlockSpec(memory_space=pl.ANY)
    return pl.pallas_call(
        functools.partial(kernel, ranks, count),
        out_shape=jax.ShapeDtypeStruct((heads * width, length), bf16),
        in_specs=[pl.BlockSpec(memory_space=pltpu.SMEM)] + [away] * 4 + [here] * 3,
        out_specs=here,
        scratch_shapes=[
            VMEM((ranks,) + features.shape, bf16),
            VMEM((3,) + w_query.shape, bf16),
            VMEM((heads * width, length), bf16),
            VMEM((heads, blocks, 3, width, wide), jnp.float32),
            VMEM((2, heads, width, wide), jnp.float32),
            VMEM((2, heads, width, wide), bf16),
            VMEM((2, heads, width, width), jnp.float32),
            VMEM((heads, width, wide), jnp.float32),
            VMEM((rounds, heads, width, wide), bf16),
            VMEM((rounds + 1, heads, width, wide), bf16),
            VMEM((2, heads, width // 2, wide), bf16),
            VMEM((2, heads, width // 2, wide), bf16),
            pltpu.SemaphoreType.DMA((4,)),
            pltpu.SemaphoreType.DMA((40,)),
            pltpu.SemaphoreType.DMA((40,)),
            pltpu.SemaphoreType.DMA((rounds + 3,)),
            pltpu.SemaphoreType.DMA((rounds + 3,)),
        ],
        compiler_params=pltpu.CompilerParams(
            collective_id=0, has_side_effects=True, vmem_limit_bytes=58 << 20
        ),
        name="ttt_layer",
    )(scene_bounds, features, w_query, w_key, w_value, rates.T, w_init, out_gain[None, :])


def solution(mesh):
    return jax.shard_map(
        functools.partial(on_device, mesh.shape["head"], mesh.shape["seq"]),
        mesh=mesh,
        in_specs=(
            P("head", "seq"),
            P("head", None),
            P("head", None),
            P("head", None),
            P("seq", "head"),
            P("seq", None),
            P("head", None, None),
            P("head"),
        ),
        out_specs=P("head", "seq"),
        check_vma=False,
    )
```

```python
import functools
import math

import jax
import jax.numpy as jnp
from jax import lax
from jax.experimental import pallas as pl
from jax.experimental.pallas import tpu as pltpu
from jax.sharding import PartitionSpec as P

MINI = 64
MESH = pl.DeviceIdType.MESH
VMEM = pltpu.VMEM
bf16 = jnp.bfloat16


def dot(a, b):
    return jnp.dot(a.astype(bf16), b.astype(bf16), preferred_element_type=jnp.float32)


def split(a):
    high = a.astype(bf16)
    return high, (a - high.astype(jnp.float32)).astype(bf16)


def dot_left(a, b):
    high, rest = split(a)
    return dot(high, b) + dot(rest, b)


def dot_right(a, b):
    high, rest = split(b)
    return dot(a, high) + dot(a, rest)


def dot_both(a, b):
    high, rest = split(a)
    return dot_right(high, b) + dot(rest, b)


def iota2(shape, axis):
    return lax.broadcasted_iota(jnp.int32, shape, axis)


def eye_at(rows, cols, shift):
    return (iota2((rows, cols), 1) == iota2((rows, cols), 0) + shift).astype(jnp.float32)


def stack(upper, lower):
    return jnp.concatenate([upper, lower.astype(upper.dtype)], axis=0)


def pack(state):
    half = state.shape[0] // 2
    return jnp.concatenate([state[:half], state[half:]], axis=1)


def unpack(packed):
    width = packed.shape[1] // 2
    return jnp.concatenate([packed[:, :width], packed[:, width:]], axis=0)


def remote(src, dst, sems, index, peer):
    return pltpu.make_async_remote_copy(
        src_ref=src,
        dst_ref=dst,
        send_sem=sems[0].at[index],
        recv_sem=sems[1].at[index],
        device_id=peer,
        device_id_type=MESH,
    )


def spread(side, me, x_ref, gathered, sems):
    own_x, own_y = lax.rem(me, side), me // side
    half_rows = x_ref.shape[0] // 2
    sent = []

    def wrap(place):
        return lax.rem(place + 2 * side, side)

    def index(half, u, w):
        return wrap(w) * side + wrap(u) if half == 0 else wrap(u) * side + wrap(w)

    def rows(half, piece):
        if piece is None:
            return pl.ds(half * half_rows, half_rows)
        return pl.ds(half * half_rows + piece * (half_rows // 2), half_rows // 2)

    def slot(half, u, w, piece=None):
        return gathered.at[index(half, u, w), rows(half, piece)]

    def place(half):
        return (own_x, own_y) if half == 0 else (own_y, own_x)

    def send(half, number, source, target, peer):
        copy = remote(source, target, sems, 20 * half + number, {"head": peer})
        copy.start()
        sent.append(copy)

    def arrive(half, number, target):
        remote(target, target, sems, 20 * half + number, {"head": index(half, *place(half))}).wait_recv()

    def along(half, axis, hop):
        u, w = place(half)
        return index(half, u + hop, w) if axis == 0 else index(half, u, w + hop)

    def open_stream(half, axis, base, u, w, source, direct):
        for number, hop in ((0, 1), (1, -1), (2, 2))[: 3 if direct else 2]:
            send(half, base + number, source, slot(half, u, w), along(half, axis, hop))

    def relay(half, axis, base, u, w, direct):
        for number, hop in ((0, 1), (1, -1)):
            au, aw = (u - hop, w) if axis == 0 else (u, w - hop)
            arrive(half, base + number, slot(half, au, aw))
            if not direct:
                block = slot(half, au, aw, number)
                send(half, base + 2 + number, block, block, along(half, axis, hop))
            if axis == 0:
                whole = slot(half, au, aw)
                open_stream(half, 1, 8 + 4 * number, au, aw, whole, False)

    def close(half, axis, base, u, w, direct):
        au, aw = (u + 2, w) if axis == 0 else (u, w + 2)
        if direct:
            arrive(half, base + 2, slot(half, au, aw))
        else:
            for number in range(2):
                arrive(half, base + 2 + number, slot(half, au, aw, number))
        if axis == 0:
            open_stream(half, 1, 16, au, aw, slot(half, au, aw), True)

    def own(half):
        return x_ref.at[rows(half, None)]

    halves = range(2)
    for half in halves:
        open_stream(half, 0, 0, *place(half), own(half), True)
    for half in halves:
        open_stream(half, 1, 4, *place(half), own(half), False)
    for half in halves:
        relay(half, 0, 0, *place(half), True)
    for half in halves:
        close(half, 0, 0, *place(half), True)
    shifts = (0, -1, 1, 2)
    for step in range(5):
        for half in halves:
            u, w = place(half)
            if step < 4:
                relay(half, 1, 4 + 4 * step, u + shifts[step], w, step == 3)
            if step > 0:
                close(half, 1, 4 * step, u + shifts[step - 1], w, step == 4)
    return sent


def unit(rows):
    scale = lax.rsqrt(jnp.mean(rows * rows, axis=0, keepdims=True) + 1e-06)
    return rows * scale / math.sqrt(rows.shape[0])


def local_maps(heads, width, live, keys, values, rates_ref, terms, maps, maps_low):
    length = keys.shape[1]
    blocks = length // MINI
    eta = rates_ref[...] * live
    eye = eye_at(width, 2 * width, 0)
    low = eye_at(width, 2 * width, width)
    kept = []
    for h in range(heads):
        part = slice(h * width, (h + 1) * width)
        key_t = unit(keys[part])
        gain_t = (key_t * eta[h : h + 1]).astype(bf16)
        kv = jnp.concatenate([-key_t, values[part]], axis=0).T.astype(bf16)
        kept.append((gain_t, kv))
        pairs = []
        for n in range(blocks):
            span = slice(n * MINI, (n + 1) * MINI)
            pair = dot(gain_t[:, span], kv[span])
            terms[h, n, 2] = pair
            pairs.append(pair)
        for way in range(2):
            order = pairs if way == 0 else pairs[::-1]
            total = order[0] + eye
            for pair in order[1:]:
                total = total + dot_left(pair, stack(total, low))
            maps[way, h] = total
            maps_low[way, h] = total.astype(bf16)
    return kept


def local_outputs(h, query_t, gain_t, kv, terms):
    blocks = query_t.shape[1] // MINI
    rows = iota2((MINI, MINI), 0)
    cols = iota2((MINI, MINI), 1)
    q = unit(query_t).T
    for n in range(blocks):
        span = slice(n * MINI, (n + 1) * MINI)
        scores = dot(q[span], gain_t[:, span])
        left = jnp.concatenate([jnp.where(cols <= rows, scores, 0.0), jnp.where(cols >= rows, scores, 0.0)], axis=0)
        both = dot(left, kv[span])
        q_wide = jnp.concatenate([q[span], jnp.zeros_like(q[span])], axis=1)
        terms[h, n, 0] = both[:MINI] + q_wide
        terms[h, n, 1] = both[MINI:] + q_wide


def prefix(count, maps, maps_low, w_ref, entry, cur, out_maps, got, states, got_states, sems, peers, fills):
    heads, width = w_ref.shape[0], w_ref.shape[1]
    core, order, steps, far, other, ring = peers
    low = eye_at(width, 2 * width, width)
    eye = eye_at(width, width, 0)
    copies = []

    def move(index, src, dst, peer):
        copy = remote(src, dst, sems, index, {"seq": peer})
        copy.start()
        copies.append(copy)
        return copy

    def fill():
        if fills:
            fills.pop(0)()

    first = move(0, maps_low.at[1 - core], got.at[0], other)
    fill()
    first.wait_recv()
    for h in range(heads):
        total = dot_right(got[0, h], stack(maps[core, h], low))
        cur[h] = total
        out_maps[0, h] = total.astype(bf16)
    for i, hop in enumerate(steps):
        copy = move(i + 1, out_maps.at[i], got.at[i + 1], ring(hop))
        fill()
        copy.wait_recv()
        keep = order >= hop
        for h in range(heads):
            mine = cur[h]
            total = jnp.where(keep, dot_left(mine, stack(got[i + 1, h], low)), mine)
            cur[h] = total
            out_maps[i + 1, h] = total.astype(bf16)
    base = len(steps)
    for h in range(heads):
        states[0, h] = pack(dot_both(cur[h], stack(w_ref[h], eye))).astype(bf16)
    ahead = move(base + 2, states.at[0], got_states.at[0], ring(far))
    near = move(base + 1, out_maps.at[base], got.at[base + 1], ring(1))
    while fills:
        fill()
    near.wait_recv()
    ahead.wait_recv()
    for h in range(heads):
        start = w_ref[h]
        before = jnp.where(order >= far, unpack(got_states[0, h].astype(jnp.float32)), start)
        state = jnp.where(order >= 1, dot_right(got[base + 1, h], stack(before, eye)), start)
        entry[core, h] = state
        states[1, h] = pack(dot_both(maps[core, h], stack(state, eye))).astype(bf16)
    move(base + 3, states.at[1], got_states.at[1], other).wait_recv()
    for h in range(heads):
        entry[1 - core, h] = unpack(got_states[1, h].astype(jnp.float32))
    for copy in copies:
        copy.wait_send()


def finish(heads, width, live, terms, entry, gain_ref, out_ref):
    blocks = terms.shape[1]
    eye = eye_at(width, width, 0)

    def norm(values):
        centre = values - jnp.mean(values, axis=0, keepdims=True)
        return centre * lax.rsqrt(jnp.mean(centre * centre, axis=0, keepdims=True) + 1e-05)

    gain = jnp.broadcast_to(gain_ref[...], (8, heads * width)).T[:, :1]
    rows = {}
    states = {(h, way): entry[way, h] for h in range(heads) for way in range(2)}
    for step in range(blocks):
        for h in range(heads):
            for way in range(2):
                n = step if way == 0 else blocks - 1 - step
                state = states[h, way]
                left = jnp.concatenate([terms[h, n, way], terms[h, n, 2]], axis=0)
                both = dot_both(left, stack(state, eye))
                rows[h, way, n] = both[:MINI]
                states[h, way] = state + both[MINI:]
    for h in range(heads):
        total = 0.0
        for way in range(2):
            total = total + norm(jnp.concatenate([rows[h, way, n] for n in range(blocks)], axis=0).T)
        part = pl.ds(h * width, width)
        out_ref[part, :] = (total * gain[h * width : (h + 1) * width] * live).astype(out_ref.dtype)


def kernel(
    ranks, count, bounds_ref, x_ref, wq_ref, wk_ref, wv_ref, rates_ref, w_ref, gain_ref, out_ref,
    gathered, weights, queries, terms, maps, maps_low, entry, cur, out_maps, got, states, got_states,
    local_sem, gather_send, gather_recv, send_sem, recv_sem,
):
    heads, width = w_ref.shape[0], w_ref.shape[1]
    length = x_ref.shape[1]
    me = lax.axis_index("head")
    place = lax.axis_index("seq")
    chips = count // 2
    core = lax.rem(place, 2)
    chip = place // 2
    sign = 1 - 2 * core
    steps = []
    hop = 1
    while 2 * hop < chips:
        steps.append(hop)
        hop *= 2
    far = hop + 1
    other = place + sign
    order = chip * (1 - core) + (chips - 1 - chip) * core

    def ring(hops):
        return lax.rem(chip + sign * hops + 2 * chips, chips) * 2 + core

    barrier = pltpu.get_barrier_semaphore()
    greet = [{"seq": other}]
    for hops in steps:
        greet += [{"seq": ring(hops)}, {"seq": ring(-hops)}]
    side = math.isqrt(ranks)
    own_x, own_y = lax.rem(me, side), me // side
    if side > 1:
        for hop in (1, side - 1, 2):
            greet.append({"head": own_y * side + lax.rem(own_x + hop, side)})
            greet.append({"head": lax.rem(own_y + hop, side) * side + own_x})
    for peer in greet:
        pl.semaphore_signal(barrier, inc=1, device_id=peer, device_id_type=MESH)
    loads = [pltpu.make_async_copy(x_ref, gathered.at[me], local_sem.at[0])]
    for i, ref in enumerate((wq_ref, wk_ref, wv_ref)):
        loads.append(pltpu.make_async_copy(ref, weights.at[i], local_sem.at[i + 1]))
    for load in loads:
        load.start()
    pl.semaphore_wait(barrier, len(greet))

    sent = []
    if side > 1:
        sent = spread(side, me, x_ref, gathered, (gather_send, gather_recv))
    for load in loads:
        load.wait()
    piece = gathered[...].reshape(-1, length)

    def project(i):
        total = jnp.dot(weights[i], piece, preferred_element_type=jnp.float32)
        return total.astype(bf16).astype(jnp.float32)

    slots = iota2((1, length), 1)
    live = ((slots >= bounds_ref[0, 0]) & (slots < bounds_ref[0, 1])).astype(jnp.float32)
    kept = local_maps(heads, width, live, project(1), project(2), rates_ref, terms, maps, maps_low)

    def query_fill():
        queries[...] = jnp.dot(weights[0], gathered[...].reshape(-1, length), preferred_element_type=jnp.float32).astype(bf16)

    def output_fill(h):
        local_outputs(h, queries[pl.ds(h * width, width), :].astype(jnp.float32), *kept[h], terms)

    fills = [query_fill] + [functools.partial(output_fill, h) for h in range(heads)]
    peers = (core, order, steps, far, other, ring)
    prefix(count, maps, maps_low, w_ref, entry, cur, out_maps, got, states, got_states, (send_sem, recv_sem), peers, fills)
    finish(heads, width, live, terms, entry, gain_ref, out_ref)
    for copy in sent:
        copy.wait_send()


def on_device(ranks, count, features, w_query, w_key, w_value, rates, scene_bounds, w_init, out_gain):
    length = features.shape[1]
    heads, width = w_init.shape[0], w_init.shape[1]
    wide = 2 * width
    blocks = length // MINI
    rounds = max(1, int(math.log2(count // 2)))
    here = pl.BlockSpec(memory_space=VMEM)
    away = pl.BlockSpec(memory_space=pl.ANY)
    return pl.pallas_call(
        functools.partial(kernel, ranks, count),
        out_shape=jax.ShapeDtypeStruct((heads * width, length), bf16),
        in_specs=[pl.BlockSpec(memory_space=pltpu.SMEM)] + [away] * 4 + [here] * 3,
        out_specs=here,
        scratch_shapes=[
            VMEM((ranks,) + features.shape, bf16),
            VMEM((3,) + w_query.shape, bf16),
            VMEM((heads * width, length), bf16),
            VMEM((heads, blocks, 3, width, wide), jnp.float32),
            VMEM((2, heads, width, wide), jnp.float32),
            VMEM((2, heads, width, wide), bf16),
            VMEM((2, heads, width, width), jnp.float32),
            VMEM((heads, width, wide), jnp.float32),
            VMEM((rounds, heads, width, wide), bf16),
            VMEM((rounds + 1, heads, width, wide), bf16),
            VMEM((2, heads, width // 2, wide), bf16),
            VMEM((2, heads, width // 2, wide), bf16),
            pltpu.SemaphoreType.DMA((4,)),
            pltpu.SemaphoreType.DMA((40,)),
            pltpu.SemaphoreType.DMA((40,)),
            pltpu.SemaphoreType.DMA((rounds + 3,)),
            pltpu.SemaphoreType.DMA((rounds + 3,)),
        ],
        compiler_params=pltpu.CompilerParams(
            collective_id=0, has_side_effects=True, vmem_limit_bytes=58 << 20
        ),
        name="ttt_layer",
    )(scene_bounds, features, w_query, w_key, w_value, rates.T, w_init, out_gain[None, :])


def solution(mesh):
    return jax.shard_map(
        functools.partial(on_device, mesh.shape["head"], mesh.shape["seq"]),
        mesh=mesh,
        in_specs=(
            P("head", "seq"),
            P("head", None),
            P("head", None),
            P("head", None),
            P("seq", "head"),
            P("seq", None),
            P("head", None, None),
            P("head"),
        ),
        out_specs=P("head", "seq"),
        check_vma=False,
    )
```
